32 devices in a mesh: groups: 2 (over y), lib: 4 (over z), tmpl: 2 (over x), sub: 2 (over core).
Axes of the slice: x: 2, y: 2, z: 4, core: 2. Of those that a mesh axis runs over, the one named last changes fastest.
Arguments:
- coords: float32 [512, 3, 128], P(('groups', 'lib', 'tmpl')), parts along dimension 0, may hold values from -5 to 5
- atom_type: int32 [512, 128], P(('groups', 'lib', 'tmpl')), parts along dimension 0, may hold values from 0 to 15
- channel: int32 [512, 128], P(('groups', 'lib', 'tmpl')), parts along dimension 0, may hold values from 0 to 2
- charge: float32 [512, 128], P(('groups', 'lib', 'tmpl')), parts along dimension 0, may hold values from -3 to 3
- pair_owner: int32 [512, 4], P(('groups', 'lib', 'tmpl')), parts along dimension 0, may hold values from 0 to 7, all different within a row; in each aligned block of 32 rows (0 to 31, 32 to 63, ...) at most 32 rows name the same one
- pair_slot: int32 [512, 4], P(('groups', 'lib', 'tmpl')), parts along dimension 0, may hold values from 0 to 511
- type_table: float32 [16, 2], replicated, may hold values from 0.3 to 3
- widths: float32 [5], replicated, may hold values from 0.3 to 1.2
- tmpl_points: float32 [4096, 3, 256], P(('lib', 'tmpl'), None, 'sub'), may hold values from -5 to 5
- tmpl_weights: bfloat16 [4096, 5, 256], P(('lib', 'tmpl'), None, 'sub'), may hold values from -3 to 3
Outputs:
- scores: float32 [512, 4], P(('groups', 'lib', 'tmpl')), parts along dimension 0
- pose_grad: float32 [512, 12], P(('groups', 'lib', 'tmpl')), parts along dimension 0
- weight_grad: float32 [8192, 5, 256], P(('groups', 'lib', 'tmpl'), None, 'sub'), parts along dimension 0
The draws below stay inside these ranges and needn't reach their ends.
There are 2 independent parts, one for each index of `groups`. The reference program is written for one: setup_inputs(seed, part) draws one part's arguments, and reference() takes and returns one part's arrays. A program takes and returns all parts, laid end to end along the dimension named above; an argument that names none is the same for every part. Nothing has to cross between parts.
Inputs may be any that keep to these rules, and one draw needn't show every extreme that they name: `pair_owner`: each row names 4 different owners; among the 32 rows of one device (aligned blocks) no owner is named more than 32 times, a bound that some block reaches.
All inputs are finite; a program needn't handle non-finite values.
Results may differ from the reference program's by a relative error of at most 0.0003.
Values sent between devices are 32-bit elements; how exact they have to be, the bound alone decides.
A program may use at most 64 MiB of HBM per device.

```python
import math
import jax
import jax.numpy as jnp
import numpy as np
from jax import lax

A = 128
TA = 256
F = 5
NT = 16
TOP = 4
TEMPLATES = 4096
CB = 32
OWNERS = 8
CAP = 32
TMPL_DEV = 512
BLOCKS = 256


def touch_ends(array, stream_key, least, largest):
    longest = array.shape.index(max(array.shape))
    spots = []
    for shift in (0, 1):
        where = [jax.random.randint(jax.random.fold_in(stream_key, axis), (), 0, length) for axis, length in enumerate(array.shape)]
        where[longest] = (where[longest] + shift) % array.shape[longest]
        spots.append(tuple(where))
    return array.at[spots[0]].set(least).at[spots[1]].set(largest)


def shard_levels(stream_key, dims, shards, low, largest):
    gain = 1.0
    for position, parts in shards:
        heights = jax.random.uniform(jax.random.fold_in(jax.random.fold_in(stream_key, 6), position), (parts,), jnp.float32, low / len(shards), largest / len(shards))
        gain = gain * jnp.repeat(jnp.exp(heights), dims[position] // parts).reshape((-1,) + (1,) * (len(dims) - 1 - position))
    return gain


def deal_out(stream_key, own, number, rows, amount, top, limit, slope):
    ranking = jax.random.permutation(stream_key, amount)
    crowded, ordinary = portions_of(amount, rows * top, limit, slope, True), portions_of(amount, rows * top, limit, slope, False)
    places = jnp.arange(amount)

    def named(tallies, rotation):
        used = int((tallies > 0).sum())
        fixed = max(1, used // 4)
        moved = fixed + (places - fixed + rotation * (used - fixed)) % max(1, amount - fixed)
        return jnp.zeros((amount,), jnp.int32).at[ranking[jnp.where(places < fixed, places, moved)]].set(jnp.asarray(tallies, jnp.int32))

    tallies = jnp.where(number % 4 == 0, named(crowded, number // 4), named(ordinary, number - number // 4 - 1))
    mixed = jax.random.permutation(jax.random.fold_in(own, 3), amount)
    giver, receiver = mixed[0:amount // 2 * 2:2], mixed[1:amount // 2 * 2:2]
    margin = jnp.minimum(tallies[giver] - 1, limit - tallies[receiver]) // 2
    margin = jnp.where((giver == ranking[0]) | (receiver == ranking[0]) | (tallies[receiver] == 0), 0, jnp.maximum(margin, 0))
    moved = jax.random.randint(jax.random.fold_in(own, 4), (amount // 2,), 0, 1 << 20) % (margin + 1)
    tallies = tallies.at[giver].add(-moved).at[receiver].add(moved)
    members = jnp.searchsorted(jnp.cumsum(tallies), jnp.arange(rows * top), side="right").astype(jnp.int32)
    listing = members.reshape(top, rows).T
    listing = listing[jax.random.permutation(jax.random.fold_in(own, 1), rows)]
    rotation = jax.random.randint(jax.random.fold_in(own, 2), (rows, 1), 0, top)
    return jnp.take_along_axis(listing, (jnp.arange(top)[None, :] + rotation) % top, axis=1)


def portions_of(amount, total, bound, lean, full):
    loads = [(1 << 20) // math.isqrt(standing ** lean) + 1 for standing in range(1, amount + 1)]
    largest = bound if full else min(bound, max(-(-total // amount), total * loads[0] // sum(loads)))
    least = 1 if total - largest >= amount - 1 else 0
    holding, spare = [largest] + [least] * (amount - 1), total - largest - least * (amount - 1)
    while spare > 0:
        free = [i for i in range(1, amount) if holding[i] < largest] or [i for i in range(1, amount) if holding[i] < bound]
        pool, remaining = sum([loads[i] for i in free]), spare
        for i in free:
            extra = min(bound - holding[i], max(1, remaining * loads[i] // pool), spare)
            holding[i] = holding[i] + extra
            spare = spare - extra
    return np.array(holding)


def centred(rng, shape, scale, limit, split=(), kind=jnp.bfloat16):
    array = jax.random.normal(rng, shape, jnp.float32) * scale
    if len(split) > 0:
        array = shard_levels(rng, shape, split, -0.22, 0.18) * array
    return jnp.clip(array, min=-limit, max=limit).astype(kind)


def setup_inputs(seed: int = 0, part: int = 0) -> dict:
    key_of = jax.random.split(jax.random.key(seed), 11)
    part_keys = jax.random.split(jax.random.fold_in(key_of[10], part), 11)
    coords = centred(part_keys[0], (BLOCKS, 3, A), 1.0, 5.0, ((0, 8),), jnp.float32)
    atom_type = touch_ends(jax.random.randint(part_keys[1], (BLOCKS, A), 0, NT), jax.random.fold_in(part_keys[1], 1), 0, NT - 1).astype(jnp.int32)
    channel = touch_ends(jax.random.randint(part_keys[2], (BLOCKS, A), 0, 3), jax.random.fold_in(part_keys[2], 1), 0, 2).astype(jnp.int32)
    charge = centred(part_keys[3], (BLOCKS, A), 0.5, 3.0, ((0, 8),), jnp.float32)
    pair_owner_keys = jax.random.split(jax.random.fold_in(part_keys[4], 1), BLOCKS // CB)
    pair_owner_turns = jax.random.permutation(jax.random.fold_in(part_keys[4], 3), BLOCKS // CB)
    pair_owner = jax.vmap(lambda own, number: deal_out(jax.random.fold_in(part_keys[4], 2), own, number, CB, OWNERS, TOP, CAP, 2))(pair_owner_keys, pair_owner_turns).reshape((BLOCKS, TOP))
    pair_slot = touch_ends(jax.random.randint(part_keys[5], (BLOCKS, TOP), 0, TMPL_DEV), jax.random.fold_in(part_keys[5], 1), 0, TMPL_DEV - 1).astype(jnp.int32)
    type_table = jnp.clip(jnp.exp(jax.random.uniform(key_of[6], (NT, 2), jnp.float32, math.log(0.3), math.log(3.0))), 0.3, 3.0)
    widths = jnp.clip(jnp.exp(jax.random.uniform(key_of[7], (F,), jnp.float32, math.log(0.3), math.log(1.2))), 0.3, 1.2)
    tmpl_points = centred(key_of[8], (TEMPLATES, 3, TA), 1.0, 5.0, ((0, 8), (2, 2)), jnp.float32)
    tmpl_weights = centred(key_of[9], (TEMPLATES, F, TA), 0.5, 3.0, ((0, 8), (2, 2)))
    return dict(coords=coords, atom_type=atom_type, channel=channel, charge=charge, pair_owner=pair_owner, pair_slot=pair_slot, type_table=type_table, widths=widths, tmpl_points=tmpl_points, tmpl_weights=tmpl_weights)


def atom_weights(atom_type, channel, charge, type_table):
    type_ids = jnp.arange(type_table.shape[0], dtype=jnp.int32)
    onehot = (atom_type[:, None, :] == type_ids[None, :, None]).astype(jnp.float32)
    steric = jnp.sum(onehot * type_table[None, :, 0:1], axis=1)
    strength = jnp.sum(onehot * type_table[None, :, 1:2], axis=1)
    channels = jnp.arange(3, dtype=jnp.int32)
    pharm_part = (channel[:, None, :] == channels[None, :, None]).astype(jnp.float32) * strength[:, None, :]
    return jnp.concatenate([steric[:, None, :], charge[:, None, :], pharm_part], axis=1)


def pair_terms(posed_xyz, atom_w, points, values, widths):
    offsets = posed_xyz[:, None, :] - points[:, :, None]
    sq_dist = jnp.sum(offsets * offsets, axis=0)
    kernel = jnp.exp(-widths[:, None, None] * sq_dist[None, :, :])
    crossed = kernel * atom_w[:, None, :]
    fields = crossed * values[:, :, None]
    intersection = jnp.sum(fields)
    scaled = jnp.sum(fields * (-2.0 * widths)[:, None, None], axis=0)
    forces = jnp.sum(scaled[None, :, :] * offsets, axis=1)
    shift_grad = jnp.sum(forces, axis=1)
    linear = jnp.sum(forces[:, None, :] * posed_xyz[None, :, :], axis=2).reshape(9)
    weight_part = jnp.sum(crossed, axis=2)
    return jnp.concatenate([intersection[None], shift_grad, linear]), weight_part


def reference(coords, atom_type, channel, charge, pair_owner, pair_slot, type_table, widths, tmpl_points, tmpl_weights):
    atom_w = atom_weights(atom_type, channel, charge, type_table)
    tmpl_w = tmpl_weights.astype(jnp.float32)
    templates = (pair_owner * TMPL_DEV + pair_slot).astype(jnp.int32)

    def advance(running, element):
        posed_xyz, block_w, tmpl_ids = element

        def single(tmpl_id):
            points = lax.dynamic_index_in_dim(tmpl_points, tmpl_id, 0, keepdims=False)
            values = lax.dynamic_index_in_dim(tmpl_w, tmpl_id, 0, keepdims=False)
            return pair_terms(posed_xyz, block_w, points, values, widths)

        results, weight_part = lax.map(single, tmpl_ids)
        running = running.at[tmpl_ids].add(weight_part)
        return running, results

    initial = jnp.zeros((TEMPLATES, F, TA), jnp.float32)
    weight_grad, results = lax.scan(advance, initial, (coords, atom_w, templates))
    scores = results[:, :, 0]
    pose_grad = jnp.sum(results[:, :, 1:], axis=1)
    return (scores, pose_grad, weight_grad)
```

```python
import functools
import math

import jax
import jax.numpy as jnp
from jax import lax
from jax.experimental import pallas as pl
from jax.experimental.pallas import tpu as pltpu
from jax.sharding import PartitionSpec as P

MESH = pl.DeviceIdType.MESH
F32 = jnp.float32
BF16 = jnp.bfloat16
GROUP = 4
VALUES = 16


def gather_kernel(libs, tmpls, own_ref, all_ref, local_sem, z_send, z_recv, x_send, x_recv, s_send, s_recv):
    l = lax.axis_index("lib")
    t = lax.axis_index("tmpl")
    s = lax.axis_index("sub")
    half = own_ref.shape[0] // 2
    barrier = pltpu.get_barrier_semaphore()

    @pl.loop(1, libs)
    def _(k):
        pl.semaphore_signal(barrier, inc=1, device_id={"lib": lax.rem(l + k, libs)}, device_id_type=MESH)

    @pl.loop(1, tmpls)
    def _(k):
        pl.semaphore_signal(barrier, inc=1, device_id={"tmpl": lax.rem(t + k, tmpls)}, device_id_type=MESH)

    pl.semaphore_signal(barrier, inc=1, device_id={"sub": 1 - s}, device_id_type=MESH)
    mine = own_ref.at[pl.ds(s * half, half)]
    local = pltpu.make_async_copy(own_ref, all_ref.at[l, t], local_sem)
    pl.semaphore_wait(barrier, libs + tmpls - 1)
    local.start()

    def z_copy(k):
        return pltpu.make_async_remote_copy(
            src_ref=mine, dst_ref=all_ref.at[l, t, pl.ds(s * half, half)], send_sem=z_send.at[k], recv_sem=z_recv.at[k],
            device_id={"lib": lax.rem(l + k, libs)}, device_id_type=MESH)

    def x_copy(k, m, src):
        return pltpu.make_async_remote_copy(
            src_ref=src, dst_ref=all_ref.at[lax.rem(l - k + libs, libs), t, pl.ds(s * half, half)],
            send_sem=x_send.at[k, m], recv_sem=x_recv.at[k, m],
            device_id={"tmpl": lax.rem(t + m, tmpls)}, device_id_type=MESH)

    def s_copy(k, m):
        spot = all_ref.at[lax.rem(l - k + libs, libs), lax.rem(t - m + tmpls, tmpls), pl.ds(s * half, half)]
        return pltpu.make_async_remote_copy(
            src_ref=spot, dst_ref=spot, send_sem=s_send.at[k, m], recv_sem=s_recv.at[k, m],
            device_id={"sub": 1 - s}, device_id_type=MESH)

    @pl.loop(1, tmpls)
    def _(m):
        x_copy(0, m, mine).start()

    @pl.loop(1, libs)
    def _(k):
        z_copy(k).start()

    @pl.loop(1, libs)
    def _(k):
        z_copy(k).wait_recv()
        spot = all_ref.at[lax.rem(l - k + libs, libs), t, pl.ds(s * half, half)]

        @pl.loop(1, tmpls)
        def _(m):
            x_copy(k, m, spot).start()

        s_copy(k, 0).start()

    @pl.loop(1, tmpls)
    def _(m):
        @pl.loop(0, libs)
        def _(k):
            x_copy(k, m, mine).wait_recv()
            s_copy(k, m).start()

    local.wait()

    @pl.loop(1, libs)
    def _(k):
        z_copy(k).wait_send()
        s_copy(k, 0).wait()

    @pl.loop(1, tmpls)
    def _(m):
        @pl.loop(0, libs)
        def _(k):
            x_copy(k, m, mine).wait_send()
            s_copy(k, m).wait()


def gather_blocks(payload, libs, tmpls):
    dma = pltpu.SemaphoreType.DMA
    return pl.pallas_call(
        functools.partial(gather_kernel, libs, tmpls),
        out_shape=jax.ShapeDtypeStruct((libs, tmpls) + payload.shape, F32),
        in_specs=[pl.BlockSpec(memory_space=pltpu.VMEM)],
        out_specs=pl.BlockSpec(memory_space=pltpu.VMEM),
        scratch_shapes=[dma, dma((libs,)), dma((libs,)), dma((libs, tmpls)), dma((libs, tmpls)),
                        dma((libs, tmpls)), dma((libs, tmpls))],
        compiler_params=pltpu.CompilerParams(collective_id=0, has_side_effects=True, vmem_limit_bytes=60 << 20),
    )(payload)


def split3(a):
    h = a.astype(BF16).astype(F32)
    r = a - h
    m = r.astype(BF16).astype(F32)
    return h, m, r - m


def split2(a):
    h = a.astype(BF16)
    return h, (a - h.astype(F32)).astype(BF16)


def pair_kernel(per_dev, slot_ref, widths_ref, blocks_ref, points_ref, weights_ref, wg_ref, out_ref, res_ref):
    devices = blocks_ref.shape[0]
    wg_ref[...] = jnp.zeros_like(wg_ref)
    res_ref[...] = jnp.zeros_like(res_ref)
    row = lax.broadcasted_iota(jnp.int32, (8, 128), 0)
    row16 = lax.broadcasted_iota(jnp.int32, (VALUES, 128), 0)
    lane16 = lax.broadcasted_iota(jnp.int32, (VALUES, 128), 1)
    low = row < 4
    log2e = math.log2(math.e)
    wide = [widths_ref[f] for f in range(5)]
    scale = [-log2e * w for w in wide]

    def one(dev, b, slot):
        valid = jnp.where(slot >= 0, F32(1), F32(0))
        slot = jnp.maximum(slot, 0)
        x = [jnp.broadcast_to(blocks_ref[dev, b, pl.ds(c, 1), :], (8, 128)) for c in range(3)]
        y = [jnp.broadcast_to(points_ref[slot, pl.ds(c, 1), :], (8, 128)) for c in range(3)]

        def rows(first, norm_row, one_row, p):
            norm = p[0] * p[0] + p[1] * p[1] + p[2] * p[2]
            v = jnp.where(row == 0, p[0] * first, jnp.where(row == 1, p[1] * first, p[2] * first))
            return jnp.where(row < 3, v, jnp.where(row == norm_row, norm, jnp.where(row == one_row, 1.0, 0.0)))

        xh, xm, xl = split3(rows(1.0, 3, 4, x))
        yh, ym, yl = split3(rows(-2.0, 4, 3, y))
        xs = jnp.concatenate([xh, xh, xh, xm, xm, xl], axis=0).astype(BF16)
        ys = jnp.concatenate([yh, ym, yl, yh, ym, yh], axis=0).astype(BF16)
        dist = lax.dot_general(ys, xs, (((0,), (0,)), ((), ())), preferred_element_type=F32)
        chan = blocks_ref[dev, b, pl.ds(6, 1), :]
        steric = blocks_ref[dev, b, pl.ds(3, 1), :] * valid
        charge = blocks_ref[dev, b, pl.ds(4, 1), :] * valid
        strength = blocks_ref[dev, b, pl.ds(5, 1), :] * valid
        pharm_scale = jnp.where(chan == 0.0, scale[2], jnp.where(chan == 1.0, scale[3], scale[4]))
        inner = jnp.where(row % 4 == 0, 1.0, jnp.where(row % 4 == 1, x[0], jnp.where(row % 4 == 2, x[1], x[2])))
        outer = jnp.concatenate([jnp.where(low, 1.0, x[0]), jnp.where(low, x[1], x[2])], axis=0)
        moments = outer * jnp.concatenate([inner, inner], axis=0)

        def contract(exps, coefs):
            hi, lo = split2(exps)
            rhs = jnp.concatenate([hi, lo], axis=1)
            lhs = jnp.concatenate([moments * c for c in coefs], axis=0)
            lh, ll = split2(lhs)
            lhs2 = jnp.concatenate([lh, ll], axis=0)
            lhs2 = jnp.concatenate([lhs2, lhs2], axis=1)
            got = lax.dot_general(lhs2, rhs, (((1,), (1,)), ((), ())), preferred_element_type=F32)
            n = VALUES * len(coefs)
            got = got[:n] + got[n:]
            return [got[VALUES * c:VALUES * (c + 1)] for c in range(len(coefs))]

        parts = contract(jnp.exp2(dist * scale[0]), [steric]) + contract(jnp.exp2(dist * scale[1]), [charge])
        parts += contract(jnp.exp2(dist * pharm_scale),
                          [jnp.where(chan == float(c), strength, 0.0) for c in range(3)])
        vals = weights_ref[slot].astype(F32)
        total = jnp.zeros((VALUES, 128), F32)
        score = jnp.zeros((1, 128), F32)
        for f in range(5):
            v = vals[f:f + 1]
            score = score + v * parts[f][0:1]
            total = total + (v * (-2.0 * wide[f])) * parts[f]
        base = jnp.concatenate([total[0:4]] * 4, axis=0)
        y16 = jnp.concatenate([jnp.where(low, 0.0, y[0]), jnp.where(low, y[1], y[2])], axis=0)
        final = jnp.where(row16 == 0, score, total - y16 * base)
        summed = jnp.sum(final, axis=1, keepdims=True)
        wpart = jnp.concatenate([p[0:1] for p in parts], axis=0)
        return slot, wpart, summed

    group = math.gcd(GROUP, per_dev)

    @pl.loop(0, devices)
    def _(dev):
        @pl.loop(0, per_dev // group)
        def _(g):
            slots = [slot_ref[dev * per_dev + g * group + u] for u in range(group)]
            best = slots[0]
            for v in slots[1:]:
                best = jnp.maximum(best, v)

            @pl.when(best >= 0)
            def _():
                done = [one(dev, g * group + u, slots[u]) for u in range(group)]
                for u, (slot, wpart, summed) in enumerate(done):
                    wg_ref[slot] += wpart
                acc = res_ref[dev]
                for u, (slot, wpart, summed) in enumerate(done):
                    acc = jnp.where(lane16 == g * group + u, summed, acc)
                res_ref[dev] = acc

    @pl.loop(0, devices)
    def _(dev):
        r = res_ref[dev]
        packed = r[0:4]
        for q in range(1, 4):
            packed = packed + pltpu.roll(r[4 * q:4 * q + 4], 32 * q, 1)
        out_ref[dev] = packed


def run_pairs(slots, widths, blocks, points, weights):
    tmpl_count = points.shape[0]
    devices, per_dev = blocks.shape[:2]
    vmem = pl.BlockSpec(memory_space=pltpu.VMEM)
    smem = pl.BlockSpec(memory_space=pltpu.SMEM)
    return pl.pallas_call(
        functools.partial(pair_kernel, per_dev),
        out_shape=(jax.ShapeDtypeStruct((tmpl_count, 5, 128), F32), jax.ShapeDtypeStruct((devices, 4, 128), F32)),
        in_specs=[smem, smem, vmem, vmem, vmem],
        out_specs=(vmem, vmem),
        scratch_shapes=[pltpu.VMEM((devices, VALUES, 128), F32)],
        compiler_params=pltpu.CompilerParams(vmem_limit_bytes=60 << 20),
    )(slots, widths, blocks, points, weights)


def return_kernel(libs, tmpls, res_ref, owner_ref, score_ref, pose_ref, got_ref, local_sem, send_sem, recv_sem):
    l = lax.axis_index("lib")
    t = lax.axis_index("tmpl")
    s = lax.axis_index("sub")
    owners = libs * tmpls
    count = 2 * owners
    me = (l * tmpls + t) * 2 + s
    barrier = pltpu.get_barrier_semaphore()

    def peer(k):
        other = lax.rem(me + k, count)
        return other // 2, {"lib": other // (2 * tmpls), "tmpl": lax.rem(other // 2, tmpls), "sub": lax.rem(other, 2)}

    @pl.loop(1, count)
    def _(k):
        pl.semaphore_signal(barrier, inc=1, device_id=peer(k)[1], device_id_type=MESH)

    local = pltpu.make_async_copy(res_ref.at[l * tmpls + t], got_ref.at[me], local_sem)
    local.start()
    pl.semaphore_wait(barrier, count - 1)

    def copy(k):
        block, where = peer(k)
        return pltpu.make_async_remote_copy(
            src_ref=res_ref.at[block], dst_ref=got_ref.at[me], send_sem=send_sem.at[k], recv_sem=recv_sem.at[k],
            device_id=where, device_id_type=MESH)

    @pl.loop(1, count)
    def _(k):
        copy(k).start()

    local.wait()

    @pl.loop(1, count)
    def _(k):
        copy(k).wait()

    owner = owner_ref[...]

    def add(o, carry):
        total, scores = carry
        both = got_ref[2 * o] + got_ref[2 * o + 1]
        scores = jnp.where(owner == o, jnp.broadcast_to(both[0:1], (8, 128)), scores)
        return total + both, scores

    total, scores = lax.fori_loop(0, owners, add, (jnp.zeros((4, 128), F32), jnp.zeros((8, 128), F32)))
    rows = [total] + [pltpu.roll(total, 128 - 32 * q, 1) for q in range(1, 4)]
    pose = jnp.concatenate([rows[1][0:1], rows[2][0:1], rows[3][0:1], rows[1][1:4], rows[2][1:4], rows[3][1:4],
                            jnp.zeros((4, 128), F32)], axis=0)
    blocks = score_ref.shape[0]
    score_ref[...] = scores.T[:blocks, :score_ref.shape[1]]
    pose_ref[...] = pose.T[:blocks, :12]


def send_back(res, owner_rows, blocks, per_block, libs, tmpls):
    dma = pltpu.SemaphoreType.DMA
    count = 2 * libs * tmpls
    vmem = pl.BlockSpec(memory_space=pltpu.VMEM)
    return pl.pallas_call(
        functools.partial(return_kernel, libs, tmpls),
        out_shape=(jax.ShapeDtypeStruct((blocks, per_block), F32), jax.ShapeDtypeStruct((blocks, 12), F32)),
        in_specs=[vmem, vmem],
        out_specs=(vmem, vmem),
        scratch_shapes=[pltpu.VMEM((count, 4, 128), F32), dma, dma((count,)), dma((count,))],
        compiler_params=pltpu.CompilerParams(collective_id=1, has_side_effects=True),
    )(res, owner_rows)


def local(libs, tmpls, coords, atom_type, channel, charge, pair_owner, pair_slot, type_table, widths, tmpl_points,
          tmpl_weights):
    blocks, per_block = pair_owner.shape
    tmpl_count = tmpl_points.shape[0]
    types = jnp.arange(type_table.shape[0], dtype=jnp.int32)
    hot = atom_type[:, None, :] == types[None, :, None]
    steric = jnp.sum(jnp.where(hot, type_table[None, :, 0:1], 0.0), axis=1)
    strength = jnp.sum(jnp.where(hot, type_table[None, :, 1:2], 0.0), axis=1)
    names = jnp.pad((pair_owner * tmpl_count + pair_slot).astype(F32), ((0, 0), (0, 128 - per_block)))
    payload = jnp.stack([coords[:, 0], coords[:, 1], coords[:, 2], steric, charge, strength, channel.astype(F32), names],
                        axis=1)
    gathered = gather_blocks(payload, libs, tmpls).reshape(libs * tmpls, blocks, 8, 128)
    me = lax.axis_index("lib") * tmpls + lax.axis_index("tmpl")
    ids = gathered[:, :, 7, :per_block].astype(jnp.int32) - me * tmpl_count
    slots = jnp.max(jnp.where((ids >= 0) & (ids < tmpl_count), ids, -1), axis=2).reshape(-1)
    weight_grad, res = run_pairs(slots, widths, gathered, tmpl_points, tmpl_weights)
    owner_rows = jnp.pad(pair_owner.T, ((0, 8 - per_block), (0, 128 - blocks)), constant_values=-1)
    scores, pose = send_back(res, owner_rows, blocks, per_block, libs, tmpls)
    return scores, pose, weight_grad


def solution(mesh):
    every = ("groups", "lib", "tmpl")
    in_specs = (P(every, None, None), P(every, None), P(every, None), P(every, None), P(every, None), P(every, None),
                P(), P(), P(("lib", "tmpl"), None, "sub"), P(("lib", "tmpl"), None, "sub"))
    out_specs = (P(every, None), P(every, None), P(every, None, "sub"))
    body = functools.partial(local, mesh.shape["lib"], mesh.shape["tmpl"])
    return jax.shard_map(body, mesh=mesh, in_specs=in_specs, out_specs=out_specs, check_vma=False)
```

```python
import functools
import math

import jax
import jax.numpy as jnp
from jax import lax
from jax.experimental import pallas as pl
from jax.experimental.pallas import tpu as pltpu
from jax.sharding import PartitionSpec as P

MESH = pl.DeviceIdType.MESH
F32 = jnp.float32
BF16 = jnp.bfloat16
GROUP = 8
FLIP = True
VALUES = 16


def gather_kernel(libs, tmpls, xyz_ref, charge_ref, type_ref, chan_ref, owner_ref, slot_ref, real_ref, whole_ref, name_ref,
                  local_sem, z_send, z_recv, x_send, x_recv, s_send, s_recv):
    l = lax.axis_index("lib")
    t = lax.axis_index("tmpl")
    s = lax.axis_index("sub")
    half = real_ref.shape[3] // 2
    moves = [(xyz_ref, real_ref.at[l, t, pl.ds(0, 3)]), (charge_ref, real_ref.at[l, t, 3]), (type_ref, whole_ref.at[l, t, 0]),
             (chan_ref, whole_ref.at[l, t, 1]), (owner_ref, name_ref.at[l, t, 0]), (slot_ref, name_ref.at[l, t, 1])]
    moves = [pltpu.make_async_copy(src, dst, local_sem.at[n]) for n, (src, dst) in enumerate(moves)]
    for move in moves:
        move.start()
    barrier = pltpu.get_barrier_semaphore()

    @pl.loop(1, libs)
    def _(k):
        pl.semaphore_signal(barrier, inc=1, device_id={"lib": lax.rem(l + k, libs)}, device_id_type=MESH)

    @pl.loop(1, tmpls)
    def _(k):
        pl.semaphore_signal(barrier, inc=1, device_id={"tmpl": lax.rem(t + k, tmpls)}, device_id_type=MESH)

    pl.semaphore_signal(barrier, inc=1, device_id={"sub": 1 - s}, device_id_type=MESH)
    for move in moves:
        move.wait()
    pl.semaphore_wait(barrier, libs + tmpls - 1)

    def chunk(k, m):
        at = (lax.rem(l - k + libs, libs), lax.rem(t - m + tmpls, tmpls))
        part = pl.ds(s * half, half)
        return real_ref.at[at + (slice(None), part)], whole_ref.at[at + (slice(None), part)], name_ref.at[at + (s,)]

    class Bundle:
        def __init__(self, refs, send, recv, device):
            self.copies = [pltpu.make_async_remote_copy(
                src_ref=ref, dst_ref=ref, send_sem=send(n), recv_sem=recv(n), device_id=device, device_id_type=MESH)
                for n, ref in enumerate(refs)]

        def start(self):
            for c in self.copies:
                c.start()

        def wait_recv(self):
            for c in self.copies:
                c.wait_recv()

        def wait_send(self):
            for c in self.copies:
                c.wait_send()

    def z_copy(k):
        return Bundle(chunk(0, 0), lambda n: z_send.at[k, n], lambda n: z_recv.at[k, n], {"lib": lax.rem(l + k, libs)})

    def x_copy(k, m):
        return Bundle(chunk(k, 0), lambda n: x_send.at[k, m, n], lambda n: x_recv.at[k, m, n], {"tmpl": lax.rem(t + m, tmpls)})

    def s_copy(k, m):
        return Bundle(chunk(k, m), lambda n: s_send.at[k, m, n], lambda n: s_recv.at[k, m, n], {"sub": 1 - s})

    @pl.loop(1, tmpls)
    def _(m):
        x_copy(0, m).start()

    @pl.loop(1, libs)
    def _(k):
        z_copy(k).start()

    @pl.loop(1, libs)
    def _(k):
        z_copy(k).wait_recv()

        @pl.loop(1, tmpls)
        def _(m):
            x_copy(k, m).start()

        s_copy(k, 0).start()

    @pl.loop(1, tmpls)
    def _(m):
        @pl.loop(0, libs)
        def _(k):
            x_copy(k, m).wait_recv()
            s_copy(k, m).start()

    @pl.loop(1, libs)
    def _(k):
        z_copy(k).wait_send()
        s_copy(k, 0).wait_send()
        s_copy(k, 0).wait_recv()

    @pl.loop(1, tmpls)
    def _(m):
        @pl.loop(0, libs)
        def _(k):
            x_copy(k, m).wait_send()
            s_copy(k, m).wait_send()
            s_copy(k, m).wait_recv()


def gather_blocks(xyz, charge, types, chans, owners, slots, libs, tmpls):
    dma = pltpu.SemaphoreType.DMA
    blocks = charge.shape[0]
    lead = (libs, tmpls)
    vmem = pl.BlockSpec(memory_space=pltpu.VMEM)
    return pl.pallas_call(
        functools.partial(gather_kernel, libs, tmpls),
        out_shape=(jax.ShapeDtypeStruct(lead + (4, blocks, 128), F32), jax.ShapeDtypeStruct(lead + (2, blocks, 128), jnp.int32),
                   jax.ShapeDtypeStruct(lead + (2,) + owners.shape, jnp.int32)),
        in_specs=[pl.BlockSpec(memory_space=pl.ANY)] * 6,
        out_specs=(vmem,) * 3,
        scratch_shapes=[dma((6,)), dma((libs, 3)), dma((libs, 3)), dma(lead + (3,)), dma(lead + (3,)),
                        dma(lead + (3,)), dma(lead + (3,))],
        compiler_params=pltpu.CompilerParams(collective_id=0, has_side_effects=True, vmem_limit_bytes=60 << 20),
    )(xyz, charge, types, chans, owners, slots)


def split3(a):
    h = a.astype(BF16).astype(F32)
    r = a - h
    m = r.astype(BF16).astype(F32)
    return h, m, r - m


def split2(a):
    h = a.astype(BF16)
    return h, (a - h.astype(F32)).astype(BF16)


def pair_kernel(slot_ref, widths_ref, table_ref, real_ref, whole_ref, points_ref, bf_weights_ref, wg_ref, out_ref, res_ref,
                atom_ref, weights_ref):
    devices, _, per_dev, _ = real_ref.shape
    res_ref[...] = jnp.zeros_like(res_ref)
    row = lax.broadcasted_iota(jnp.int32, (8, 128), 0)
    row16 = lax.broadcasted_iota(jnp.int32, (VALUES, 128), 0)
    lane16 = lax.broadcasted_iota(jnp.int32, (VALUES, 128), 1)
    low = row < 4
    log2e = math.log2(math.e)
    wide = [widths_ref[f] for f in range(5)]
    scale = [-log2e * w for w in wide]

    @pl.loop(0, 5)
    def _(f):
        wg_ref[f] = jnp.zeros(wg_ref.shape[1:], F32)
        weights_ref[f] = bf_weights_ref[f].astype(F32)

    @pl.loop(0, devices)
    def _(dev):
        types = whole_ref[dev, 0]
        chan = whole_ref[dev, 1]
        steric = jnp.zeros(types.shape, F32)
        strength = jnp.zeros(types.shape, F32)
        for n in range(table_ref.shape[0]):
            same = types == n
            steric = jnp.where(same, table_ref[n, 0], steric)
            strength = jnp.where(same, table_ref[n, 1], strength)
        atom_ref[dev, 0] = steric
        atom_ref[dev, 1] = strength
        atom_ref[dev, 2] = jnp.where(chan == 0, scale[2], jnp.where(chan == 1, scale[3], scale[4]))

    def one(dev, b, slot):
        valid = jnp.where(slot >= 0, F32(1), F32(0))
        slot = jnp.maximum(slot, 0)
        here = pl.ds(b, 1)
        there = pl.ds(slot, 1)
        x = [jnp.broadcast_to(real_ref[dev, c, here, :], (8, 128)) for c in range(3)]
        y = [jnp.broadcast_to(points_ref[c, there, :], (8, 128)) for c in range(3)]
        chan = whole_ref[dev, 1, here, :]
        steric = atom_ref[dev, 0, here, :] * valid
        charge = real_ref[dev, 3, here, :] * valid
        strength = atom_ref[dev, 1, here, :] * valid
        pharm_scale = atom_ref[dev, 2, here, :]

        def rows(first, norm_row, one_row, p):
            norm = p[0] * p[0] + p[1] * p[1] + p[2] * p[2]
            v = jnp.where(row == 0, p[0] * first, jnp.where(row == 1, p[1] * first, p[2] * first))
            return jnp.where(row < 3, v, jnp.where(row == norm_row, norm, jnp.where(row == one_row, 1.0, 0.0)))

        def atom_side(v):
            h, m, l = split3(v)
            return jnp.concatenate([h, h, h, m, m, l], axis=0).astype(BF16)

        xv = rows(1.0, 3, 4, x)
        xs = atom_side(xv)
        yh, ym, yl = split3(rows(-2.0, 4, 3, y))
        ys = jnp.concatenate([yh, ym, yl, yh, ym, yh], axis=0).astype(BF16)
        if FLIP:
            both = jnp.concatenate([xs, atom_side(xv * pharm_scale)], axis=1)
            dist = lax.dot_general(both, ys, (((0,), (0,)), ((), ())), preferred_element_type=F32)
            dist, pharm = dist[:128], dist[128:]
        else:
            dist = lax.dot_general(ys, xs, (((0,), (0,)), ((), ())), preferred_element_type=F32)
            pharm = dist * pharm_scale
        inner = jnp.where(row % 4 == 0, 1.0, jnp.where(row % 4 == 1, x[0], jnp.where(row % 4 == 2, x[1], x[2])))
        outer = jnp.concatenate([jnp.where(low, 1.0, x[0]), jnp.where(low, x[1], x[2])], axis=0)
        moments = outer * jnp.concatenate([inner, inner], axis=0)

        def contract(exps, coefs):
            hi, lo = split2(exps)
            rhs = jnp.concatenate([hi, lo], axis=0 if FLIP else 1)
            lhs = jnp.concatenate([moments * c for c in coefs], axis=0)
            lh, ll = split2(lhs)
            lhs2 = jnp.concatenate([lh, ll], axis=0)
            lhs2 = jnp.concatenate([lhs2, lhs2], axis=1)
            got = lax.dot_general(lhs2, rhs, (((1,), (0 if FLIP else 1,)), ((), ())), preferred_element_type=F32)
            n = VALUES * len(coefs)
            got = got[:n] + got[n:]
            return [got[VALUES * c:VALUES * (c + 1)] for c in range(len(coefs))]

        parts = contract(jnp.exp2(dist * scale[0]), [steric]) + contract(jnp.exp2(dist * scale[1]), [charge])
        parts += contract(jnp.exp2(pharm), [jnp.where(chan == c, strength, 0.0) for c in range(3)])
        total = jnp.zeros((VALUES, 128), F32)
        score = jnp.zeros((1, 128), F32)
        for f in range(5):
            v = weights_ref[f, there, :]
            score = score + v * parts[f][0:1]
            total = total + (v * (-2.0 * wide[f])) * parts[f]
        base = jnp.concatenate([total[0:4]] * 4, axis=0)
        y16 = jnp.concatenate([jnp.where(low, 0.0, y[0]), jnp.where(low, y[1], y[2])], axis=0)
        final = jnp.where(row16 == 0, score, total - y16 * base)
        summed = jnp.sum(final, axis=1, keepdims=True)
        return there, [p[0:1] for p in parts], summed

    group = math.gcd(GROUP, per_dev)

    @pl.loop(0, devices)
    def _(dev):
        @pl.loop(0, per_dev // group)
        def _(g):
            slots = [slot_ref[dev, g * group + u] for u in range(group)]
            best = slots[0]
            for v in slots[1:]:
                best = jnp.maximum(best, v)

            @pl.when(best >= 0)
            def _():
                done = [one(dev, g * group + u, slots[u]) for u in range(group)]
                for there, wparts, summed in done:
                    for f, part in enumerate(wparts):
                        wg_ref[f, there, :] += part
                acc = res_ref[dev]
                for u, (there, wparts, summed) in enumerate(done):
                    acc = jnp.where(lane16 == g * group + u, summed, acc)
                res_ref[dev] = acc

    @pl.loop(0, devices)
    def _(dev):
        r = res_ref[dev]
        packed = r[0:4]
        for q in range(1, 4):
            packed = packed + pltpu.roll(r[4 * q:4 * q + 4], 32 * q, 1)
        out_ref[dev] = packed


def run_pairs(slots, widths, table, real, whole, points, weights):
    tmpl_count = points.shape[1]
    devices, _, per_dev, _ = real.shape
    vmem = pl.BlockSpec(memory_space=pltpu.VMEM)
    smem = pl.BlockSpec(memory_space=pltpu.SMEM)
    return pl.pallas_call(
        pair_kernel,
        out_shape=(jax.ShapeDtypeStruct((5, tmpl_count, 128), F32), jax.ShapeDtypeStruct((devices, 4, 128), F32)),
        in_specs=[smem, smem, smem, vmem, vmem, vmem, vmem],
        out_specs=(vmem, vmem),
        scratch_shapes=[pltpu.VMEM((devices, VALUES, 128), F32), pltpu.VMEM((devices, 3, per_dev, 128), F32),
                        pltpu.VMEM((5, tmpl_count, 128), F32)],
        compiler_params=pltpu.CompilerParams(vmem_limit_bytes=60 << 20),
    )(slots, widths, table, real, whole, points, weights)


def return_kernel(libs, tmpls, res_ref, owner_ref, score_ref, pose_ref, got_ref, local_sem, send_sem, recv_sem):
    l = lax.axis_index("lib")
    t = lax.axis_index("tmpl")
    s = lax.axis_index("sub")
    owners = libs * tmpls
    count = 2 * owners
    me = (l * tmpls + t) * 2 + s
    barrier = pltpu.get_barrier_semaphore()

    def peer(k):
        other = lax.rem(me + k, count)
        return other // 2, {"lib": other // (2 * tmpls), "tmpl": lax.rem(other // 2, tmpls), "sub": lax.rem(other, 2)}

    @pl.loop(1, count)
    def _(k):
        pl.semaphore_signal(barrier, inc=1, device_id=peer(k)[1], device_id_type=MESH)

    local = pltpu.make_async_copy(res_ref.at[l * tmpls + t], got_ref.at[me], local_sem)
    local.start()
    pl.semaphore_wait(barrier, count - 1)

    def copy(k):
        block, where = peer(k)
        return pltpu.make_async_remote_copy(
            src_ref=res_ref.at[block], dst_ref=got_ref.at[me], send_sem=send_sem.at[k], recv_sem=recv_sem.at[k],
            device_id=where, device_id_type=MESH)

    @pl.loop(1, count)
    def _(k):
        copy(k).start()

    local.wait()

    @pl.loop(1, count)
    def _(k):
        copy(k).wait()

    owner = owner_ref[...]
    per_block, blocks = owner.shape

    def add(o, carry):
        total, scores = carry
        both = got_ref[2 * o] + got_ref[2 * o + 1]
        scores = jnp.where(owner == o, jnp.broadcast_to(both[0:1, :blocks], (per_block, blocks)), scores)
        return total + both, scores

    total, scores = lax.fori_loop(0, owners, add, (jnp.zeros((4, 128), F32), jnp.zeros((per_block, blocks), F32)))
    rows = [total] + [pltpu.roll(total, 128 - 32 * q, 1) for q in range(1, 4)]
    pose = jnp.concatenate([rows[1][0:1], rows[2][0:1], rows[3][0:1], rows[1][1:4], rows[2][1:4], rows[3][1:4]], axis=0)
    score_ref[...] = scores
    pose_ref[...] = pose[:, :blocks]


def send_back(res, owner_rows, libs, tmpls):
    per_block, blocks = owner_rows.shape
    dma = pltpu.SemaphoreType.DMA
    count = 2 * libs * tmpls
    vmem = pl.BlockSpec(memory_space=pltpu.VMEM)
    return pl.pallas_call(
        functools.partial(return_kernel, libs, tmpls),
        out_shape=(jax.ShapeDtypeStruct((per_block, blocks), F32), jax.ShapeDtypeStruct((12, blocks), F32)),
        in_specs=[vmem, vmem],
        out_specs=(vmem, vmem),
        scratch_shapes=[pltpu.VMEM((count, 4, 128), F32), dma, dma((count,)), dma((count,))],
        compiler_params=pltpu.CompilerParams(collective_id=1, has_side_effects=True),
    )(res, owner_rows)


def local(libs, tmpls, coords, atom_type, channel, charge, pair_owner, pair_slot, type_table, widths, tmpl_points,
          tmpl_weights):
    owners, slots = pair_owner.T, pair_slot.T
    real, whole, names = gather_blocks(jnp.transpose(coords, (1, 0, 2)), charge, atom_type, channel, owners, slots, libs, tmpls)
    count = libs * tmpls
    real, whole, names = [a.reshape((count,) + a.shape[2:]) for a in (real, whole, names)]
    me = lax.axis_index("lib") * tmpls + lax.axis_index("tmpl")
    chosen = jnp.max(jnp.where(names[:, 0] == me, names[:, 1], -1), axis=1)
    weight_grad, res = run_pairs(chosen, widths, type_table, real, whole, jnp.transpose(tmpl_points, (1, 0, 2)),
                                 jnp.transpose(tmpl_weights, (1, 0, 2)))
    scores, pose = send_back(res, owners, libs, tmpls)
    return scores.T, pose.T, jnp.transpose(weight_grad, (1, 0, 2))


def solution(mesh):
    every = ("groups", "lib", "tmpl")
    in_specs = (P(every, None, None), P(every, None), P(every, None), P(every, None), P(every, None), P(every, None),
                P(), P(), P(("lib", "tmpl"), None, "sub"), P(("lib", "tmpl"), None, "sub"))
    out_specs = (P(every, None), P(every, None), P(every, None, "sub"))
    body = functools.partial(local, mesh.shape["lib"], mesh.shape["tmpl"])
    return jax.shard_map(body, mesh=mesh, in_specs=in_specs, out_specs=out_specs, check_vma=False)
```

```python
import functools
import math

import jax
import jax.numpy as jnp
from jax import lax
from jax.experimental import pallas as pl
from jax.experimental.pallas import tpu as pltpu
from jax.sharding import PartitionSpec as P

MESH = pl.DeviceIdType.MESH
F32 = jnp.float32
BF16 = jnp.bfloat16
GROUP = 16
FLIP = True
FLAGS = {}
VALUES = 16


def gather_kernel(libs, tmpls, xyz_ref, charge_ref, type_ref, chan_ref, owner_ref, slot_ref, real_ref, whole_ref, name_ref,
                  local_sem, z_send, z_recv, x_send, x_recv, s_send, s_recv):
    l = lax.axis_index("lib")
    t = lax.axis_index("tmpl")
    s = lax.axis_index("sub")
    half = real_ref.shape[3] // 2
    moves = [(xyz_ref, real_ref.at[l, t, pl.ds(0, 3)]), (charge_ref, real_ref.at[l, t, 3]), (type_ref, whole_ref.at[l, t, 0]),
             (chan_ref, whole_ref.at[l, t, 1]), (owner_ref, name_ref.at[l, t, 0]), (slot_ref, name_ref.at[l, t, 1])]
    moves = [pltpu.make_async_copy(src, dst, local_sem.at[n]) for n, (src, dst) in enumerate(moves)]
    for move in moves:
        move.start()
    barrier = pltpu.get_barrier_semaphore()

    @pl.loop(1, libs)
    def _(k):
        pl.semaphore_signal(barrier, inc=1, device_id={"lib": lax.rem(l + k, libs)}, device_id_type=MESH)

    @pl.loop(1, tmpls)
    def _(k):
        pl.semaphore_signal(barrier, inc=1, device_id={"tmpl": lax.rem(t + k, tmpls)}, device_id_type=MESH)

    pl.semaphore_signal(barrier, inc=1, device_id={"sub": 1 - s}, device_id_type=MESH)
    for move in moves:
        move.wait()
    pl.semaphore_wait(barrier, libs + tmpls - 1)

    def chunk(k, m):
        at = (lax.rem(l - k + libs, libs), lax.rem(t - m + tmpls, tmpls))
        part = pl.ds(s * half, half)
        return real_ref.at[at + (slice(None), part)], whole_ref.at[at + (slice(None), part)], name_ref.at[at + (s,)]

    class Bundle:
        def __init__(self, refs, send, recv, device):
            self.copies = [pltpu.make_async_remote_copy(
                src_ref=ref, dst_ref=ref, send_sem=send(n), recv_sem=recv(n), device_id=device, device_id_type=MESH)
                for n, ref in enumerate(refs)]

        def start(self):
            for c in self.copies:
                c.start()

        def wait_recv(self):
            for c in self.copies:
                c.wait_recv()

        def wait_send(self):
            for c in self.copies:
                c.wait_send()

    def z_copy(k):
        return Bundle(chunk(0, 0), lambda n: z_send.at[k, n], lambda n: z_recv.at[k, n], {"lib": lax.rem(l + k, libs)})

    def x_copy(k, m):
        return Bundle(chunk(k, 0), lambda n: x_send.at[k, m, n], lambda n: x_recv.at[k, m, n], {"tmpl": lax.rem(t + m, tmpls)})

    def s_copy(k, m):
        return Bundle(chunk(k, m), lambda n: s_send.at[k, m, n], lambda n: s_recv.at[k, m, n], {"sub": 1 - s})

    @pl.loop(1, tmpls)
    def _(m):
        x_copy(0, m).start()

    @pl.loop(1, libs)
    def _(k):
        z_copy(k).start()

    @pl.loop(1, libs)
    def _(k):
        z_copy(k).wait_recv()

        @pl.loop(1, tmpls)
        def _(m):
            x_copy(k, m).start()

        s_copy(k, 0).start()

    @pl.loop(1, tmpls)
    def _(m):
        @pl.loop(0, libs)
        def _(k):
            x_copy(k, m).wait_recv()
            s_copy(k, m).start()

    @pl.loop(1, libs)
    def _(k):
        z_copy(k).wait_send()
        s_copy(k, 0).wait_send()
        s_copy(k, 0).wait_recv()

    @pl.loop(1, tmpls)
    def _(m):
        @pl.loop(0, libs)
        def _(k):
            x_copy(k, m).wait_send()
            s_copy(k, m).wait_send()
            s_copy(k, m).wait_recv()


def gather_blocks(xyz, charge, types, chans, owners, slots, libs, tmpls):
    dma = pltpu.SemaphoreType.DMA
    blocks = charge.shape[0]
    lead = (libs, tmpls)
    vmem = pl.BlockSpec(memory_space=pltpu.VMEM)
    return pl.pallas_call(
        functools.partial(gather_kernel, libs, tmpls),
        out_shape=(jax.ShapeDtypeStruct(lead + (4, blocks, 128), F32), jax.ShapeDtypeStruct(lead + (2, blocks, 128), jnp.int32),
                   jax.ShapeDtypeStruct(lead + (2,) + owners.shape, jnp.int32)),
        in_specs=[pl.BlockSpec(memory_space=pl.ANY)] * 6,
        out_specs=(vmem,) * 3,
        scratch_shapes=[dma((6,)), dma((libs, 3)), dma((libs, 3)), dma(lead + (3,)), dma(lead + (3,)),
                        dma(lead + (3,)), dma(lead + (3,))],
        compiler_params=pltpu.CompilerParams(collective_id=0, has_side_effects=True, vmem_limit_bytes=60 << 20),
    )(xyz, charge, types, chans, owners, slots)


def split3(a):
    h = a.astype(BF16).astype(F32)
    r = a - h
    m = r.astype(BF16).astype(F32)
    return h, m, r - m


def split2(a):
    h = a.astype(BF16)
    return h, (a - h.astype(F32)).astype(BF16)


def pair_kernel(me, name_ref, widths_ref, table_ref, real_ref, whole_ref, points_ref, bf_weights_ref, wg_ref, out_ref, res_ref,
                atom_ref, weights_ref):
    devices, _, per_dev, _ = real_ref.shape
    place = me()
    res_ref[...] = jnp.zeros_like(res_ref)
    row = lax.broadcasted_iota(jnp.int32, (8, 128), 0)
    row16 = lax.broadcasted_iota(jnp.int32, (VALUES, 128), 0)
    lane16 = lax.broadcasted_iota(jnp.int32, (VALUES, 128), 1)
    low = row < 4
    log2e = math.log2(math.e)
    wide = [widths_ref[f] for f in range(5)]
    scale = [-log2e * w for w in wide]

    @pl.loop(0, 5)
    def _(f):
        wg_ref[f] = jnp.zeros(wg_ref.shape[1:], F32)
        weights_ref[f] = bf_weights_ref[f].astype(F32)

    @pl.loop(0, devices)
    def _(dev):
        types = whole_ref[dev, 0]
        chan = whole_ref[dev, 1]
        steric = jnp.zeros(types.shape, F32)
        strength = jnp.zeros(types.shape, F32)
        for n in range(table_ref.shape[1]):
            same = types == n
            steric = jnp.where(same, table_ref[0, n], steric)
            strength = jnp.where(same, table_ref[1, n], strength)
        atom_ref[dev, 0] = steric
        atom_ref[dev, 1] = strength
        atom_ref[dev, 2] = jnp.where(chan == 0, scale[2], jnp.where(chan == 1, scale[3], scale[4]))

    def one(dev, b, slot):
        valid = jnp.where(slot >= 0, F32(1), F32(0))
        slot = jnp.maximum(slot, 0)
        here = pl.ds(b, 1)
        there = pl.ds(slot, 1)
        x = [jnp.broadcast_to(real_ref[dev, c, here, :], (8, 128)) for c in range(3)]
        y = [jnp.broadcast_to(points_ref[c, there, :], (8, 128)) for c in range(3)]
        chan = whole_ref[dev, 1, here, :]
        steric = atom_ref[dev, 0, here, :] * valid
        charge = real_ref[dev, 3, here, :] * valid
        strength = atom_ref[dev, 1, here, :] * valid
        pharm_scale = atom_ref[dev, 2, here, :]

        def rows(first, norm_row, one_row, p):
            norm = p[0] * p[0] + p[1] * p[1] + p[2] * p[2]
            v = jnp.where(row == 0, p[0] * first, jnp.where(row == 1, p[1] * first, p[2] * first))
            return jnp.where(row < 3, v, jnp.where(row == norm_row, norm, jnp.where(row == one_row, 1.0, 0.0)))

        def atom_side(v):
            h, m, l = split3(v)
            return jnp.concatenate([h, h, h, m, m, l], axis=0).astype(BF16)

        xv = rows(1.0, 3, 4, x)
        xs = atom_side(xv)
        yh, ym, yl = split3(rows(-2.0, 4, 3, y))
        ys = jnp.concatenate([yh, ym, yl, yh, ym, yh], axis=0).astype(BF16)
        if FLIP:
            both = jnp.concatenate([xs, atom_side(xv * pharm_scale)], axis=1)
            dist = lax.dot_general(both, ys, (((0,), (0,)), ((), ())), preferred_element_type=F32)
            dist, pharm = dist[:128], dist[128:]
        else:
            dist = lax.dot_general(ys, xs, (((0,), (0,)), ((), ())), preferred_element_type=F32)
            pharm = dist * pharm_scale
        inner = jnp.where(row % 4 == 0, 1.0, jnp.where(row % 4 == 1, x[0], jnp.where(row % 4 == 2, x[1], x[2])))
        outer = jnp.concatenate([jnp.where(low, 1.0, x[0]), jnp.where(low, x[1], x[2])], axis=0)
        moments = outer * jnp.concatenate([inner, inner], axis=0)

        def contract(exps, coefs):
            hi, lo = split2(exps)
            rhs = jnp.concatenate([hi, lo], axis=0 if FLIP else 1)
            lhs = jnp.concatenate([moments * c for c in coefs], axis=0)
            lh, ll = split2(lhs)
            lhs2 = jnp.concatenate([lh, ll], axis=0)
            lhs2 = jnp.concatenate([lhs2, lhs2], axis=1)
            got = lax.dot_general(lhs2, rhs, (((1,), (0 if FLIP else 1,)), ((), ())), preferred_element_type=F32)
            n = VALUES * len(coefs)
            got = got[:n] + got[n:]
            return [got[VALUES * c:VALUES * (c + 1)] for c in range(len(coefs))]

        parts = contract(jnp.exp2(dist * scale[0]), [steric]) + contract(jnp.exp2(dist * scale[1]), [charge])
        parts += contract(jnp.exp2(pharm), [jnp.where(chan == c, strength, 0.0) for c in range(3)])
        total = jnp.zeros((VALUES, 128), F32)
        score = jnp.zeros((1, 128), F32)
        for f in range(5):
            v = weights_ref[f, there, :]
            score = score + v * parts[f][0:1]
            total = total + (v * (-2.0 * wide[f])) * parts[f]
        base = jnp.concatenate([total[0:4]] * 4, axis=0)
        y16 = jnp.concatenate([jnp.where(low, 0.0, y[0]), jnp.where(low, y[1], y[2])], axis=0)
        final = jnp.where(row16 == 0, score, total - y16 * base)
        summed = jnp.sum(final, axis=1, keepdims=True)
        return there, [p[0:1] for p in parts], summed

    group = math.gcd(GROUP, per_dev)

    @pl.loop(0, devices)
    def _(dev):
        @pl.loop(0, per_dev // group)
        def _(g):
            slots = []
            for u in range(group):
                slot = jnp.int32(-1)
                for k in range(name_ref.shape[2]):
                    slot = jnp.where(name_ref[dev, 0, k, g * group + u] == place, name_ref[dev, 1, k, g * group + u], slot)
                slots.append(slot)
            best = slots[0]
            for v in slots[1:]:
                best = jnp.maximum(best, v)

            @pl.when(best >= 0)
            def _():
                done = [one(dev, g * group + u, slots[u]) for u in range(group)]
                for there, wparts, summed in done:
                    for f, part in enumerate(wparts):
                        wg_ref[f, there, :] += part
                acc = res_ref[dev]
                for u, (there, wparts, summed) in enumerate(done):
                    acc = jnp.where(lane16 == g * group + u, summed, acc)
                res_ref[dev] = acc

    @pl.loop(0, devices)
    def _(dev):
        r = res_ref[dev]
        packed = r[0:4]
        for q in range(1, 4):
            packed = packed + pltpu.roll(r[4 * q:4 * q + 4], 32 * q, 1)
        out_ref[dev] = packed


def run_pairs(me, names, widths, table, real, whole, points, weights):
    tmpl_count = points.shape[1]
    devices, _, per_dev, _ = real.shape
    vmem = pl.BlockSpec(memory_space=pltpu.VMEM)
    smem = pl.BlockSpec(memory_space=pltpu.SMEM)
    return pl.pallas_call(
        functools.partial(pair_kernel, me),
        out_shape=(jax.ShapeDtypeStruct((5, tmpl_count, 128), F32), jax.ShapeDtypeStruct((devices, 4, 128), F32)),
        in_specs=[smem, smem, smem, vmem, vmem, vmem, vmem],
        out_specs=(vmem, vmem),
        scratch_shapes=[pltpu.VMEM((devices, VALUES, 128), F32), pltpu.VMEM((devices, 3, per_dev, 128), F32),
                        pltpu.VMEM((5, tmpl_count, 128), F32)],
        compiler_params=pltpu.CompilerParams(vmem_limit_bytes=60 << 20, flags=FLAGS),
    )(names, widths, table, real, whole, points, weights)


def return_kernel(libs, tmpls, res_ref, owner_ref, score_ref, pose_ref, got_ref, local_sem, send_sem, recv_sem):
    l = lax.axis_index("lib")
    t = lax.axis_index("tmpl")
    s = lax.axis_index("sub")
    owners = libs * tmpls
    count = 2 * owners
    me = (l * tmpls + t) * 2 + s
    barrier = pltpu.get_barrier_semaphore()

    def peer(k):
        other = lax.rem(me + k, count)
        return other // 2, {"lib": other // (2 * tmpls), "tmpl": lax.rem(other // 2, tmpls), "sub": lax.rem(other, 2)}

    @pl.loop(1, count)
    def _(k):
        pl.semaphore_signal(barrier, inc=1, device_id=peer(k)[1], device_id_type=MESH)

    local = pltpu.make_async_copy(res_ref.at[l * tmpls + t], got_ref.at[me], local_sem)
    local.start()
    pl.semaphore_wait(barrier, count - 1)

    def copy(k):
        block, where = peer(k)
        return pltpu.make_async_remote_copy(
            src_ref=res_ref.at[block], dst_ref=got_ref.at[me], send_sem=send_sem.at[k], recv_sem=recv_sem.at[k],
            device_id=where, device_id_type=MESH)

    @pl.loop(1, count)
    def _(k):
        copy(k).start()

    local.wait()

    @pl.loop(1, count)
    def _(k):
        copy(k).wait()

    owner = owner_ref[...]
    per_block, blocks = owner.shape

    def add(o, carry):
        total, scores = carry
        both = got_ref[2 * o] + got_ref[2 * o + 1]
        scores = jnp.where(owner == o, jnp.broadcast_to(both[0:1, :blocks], (per_block, blocks)), scores)
        return total + both, scores

    total, scores = lax.fori_loop(0, owners, add, (jnp.zeros((4, 128), F32), jnp.zeros((per_block, blocks), F32)))
    rows = [total] + [pltpu.roll(total, 128 - 32 * q, 1) for q in range(1, 4)]
    pose = jnp.concatenate([rows[1][0:1], rows[2][0:1], rows[3][0:1], rows[1][1:4], rows[2][1:4], rows[3][1:4]], axis=0)
    score_ref[...] = scores
    pose_ref[...] = pose[:, :blocks]


def send_back(res, owner_rows, libs, tmpls):
    per_block, blocks = owner_rows.shape
    dma = pltpu.SemaphoreType.DMA
    count = 2 * libs * tmpls
    vmem = pl.BlockSpec(memory_space=pltpu.VMEM)
    return pl.pallas_call(
        functools.partial(return_kernel, libs, tmpls),
        out_shape=(jax.ShapeDtypeStruct((per_block, blocks), F32), jax.ShapeDtypeStruct((12, blocks), F32)),
        in_specs=[vmem, vmem],
        out_specs=(vmem, vmem),
        scratch_shapes=[pltpu.VMEM((count, 4, 128), F32), dma, dma((count,)), dma((count,))],
        compiler_params=pltpu.CompilerParams(collective_id=1, has_side_effects=True),
    )(res, owner_rows)


def local(libs, tmpls, coords, atom_type, channel, charge, pair_owner, pair_slot, type_table, widths, tmpl_points,
          tmpl_weights):
    owners, slots = pair_owner.T, pair_slot.T
    real, whole, names = gather_blocks(jnp.transpose(coords, (1, 0, 2)), charge, atom_type, channel, owners, slots, libs, tmpls)
    count = libs * tmpls
    real, whole, names = [a.reshape((count,) + a.shape[2:]) for a in (real, whole, names)]

    def me():
        return lax.axis_index("lib") * tmpls + lax.axis_index("tmpl")

    weight_grad, res = run_pairs(me, names, widths, type_table.T, real, whole, jnp.transpose(tmpl_points, (1, 0, 2)),
                                 jnp.transpose(tmpl_weights, (1, 0, 2)))
    scores, pose = send_back(res, owners, libs, tmpls)
    return scores.T, pose.T, jnp.transpose(weight_grad, (1, 0, 2))


def solution(mesh):
    every = ("groups", "lib", "tmpl")
    in_specs = (P(every, None, None), P(every, None), P(every, None), P(every, None), P(every, None), P(every, None),
                P(), P(), P(("lib", "tmpl"), None, "sub"), P(("lib", "tmpl"), None, "sub"))
    out_specs = (P(every, None), P(every, None), P(every, None, "sub"))
    body = functools.partial(local, mesh.shape["lib"], mesh.shape["tmpl"])
    return jax.shard_map(body, mesh=mesh, in_specs=in_specs, out_specs=out_specs, check_vma=False)
```

```python
import functools
import math

import jax
import jax.numpy as jnp
from jax import lax
from jax.experimental import pallas as pl
from jax.experimental.pallas import tpu as pltpu
from jax.sharding import PartitionSpec as P

MESH = pl.DeviceIdType.MESH
F32 = jnp.float32
BF16 = jnp.bfloat16
GROUP = 32
FLIP = True
FLAGS = {}
SKEW = 2
VALUES = 16


def gather_kernel(libs, tmpls, xyz_ref, charge_ref, type_ref, chan_ref, owner_ref, slot_ref, real_ref, whole_ref, name_ref,
                  local_sem, z_send, z_recv, x_send, x_recv, s_send, s_recv):
    l = lax.axis_index("lib")
    t = lax.axis_index("tmpl")
    s = lax.axis_index("sub")
    half = real_ref.shape[3] // 2
    moves = [(xyz_ref, real_ref.at[l, t, pl.ds(0, 3)]), (charge_ref, real_ref.at[l, t, 3]), (type_ref, whole_ref.at[l, t, 0]),
             (chan_ref, whole_ref.at[l, t, 1]), (owner_ref, name_ref.at[l, t, 0]), (slot_ref, name_ref.at[l, t, 1])]
    moves = [pltpu.make_async_copy(src, dst, local_sem.at[n]) for n, (src, dst) in enumerate(moves)]
    for move in moves:
        move.start()
    barrier = pltpu.get_barrier_semaphore()

    @pl.loop(1, libs)
    def _(k):
        pl.semaphore_signal(barrier, inc=1, device_id={"lib": lax.rem(l + k, libs)}, device_id_type=MESH)

    @pl.loop(1, tmpls)
    def _(k):
        pl.semaphore_signal(barrier, inc=1, device_id={"tmpl": lax.rem(t + k, tmpls)}, device_id_type=MESH)

    pl.semaphore_signal(barrier, inc=1, device_id={"sub": 1 - s}, device_id_type=MESH)
    for move in moves:
        move.wait()
    pl.semaphore_wait(barrier, libs + tmpls - 1)

    def chunk(k, m):
        at = (lax.rem(l - k + libs, libs), lax.rem(t - m + tmpls, tmpls))
        part = pl.ds(s * half, half)
        return real_ref.at[at + (slice(None), part)], whole_ref.at[at + (slice(None), part)], name_ref.at[at + (s,)]

    class Bundle:
        def __init__(self, refs, send, recv, device):
            self.copies = [pltpu.make_async_remote_copy(
                src_ref=ref, dst_ref=ref, send_sem=send(n), recv_sem=recv(n), device_id=device, device_id_type=MESH)
                for n, ref in enumerate(refs)]

        def start(self):
            for c in self.copies:
                c.start()

        def wait_recv(self):
            for c in self.copies:
                c.wait_recv()

        def wait_send(self):
            for c in self.copies:
                c.wait_send()

    def z_copy(k):
        return Bundle(chunk(0, 0), lambda n: z_send.at[k, n], lambda n: z_recv.at[k, n], {"lib": lax.rem(l + k, libs)})

    def x_copy(k, m):
        return Bundle(chunk(k, 0), lambda n: x_send.at[k, m, n], lambda n: x_recv.at[k, m, n], {"tmpl": lax.rem(t + m, tmpls)})

    def s_copy(k, m):
        return Bundle(chunk(k, m), lambda n: s_send.at[k, m, n], lambda n: s_recv.at[k, m, n], {"sub": 1 - s})

    @pl.loop(1, tmpls)
    def _(m):
        x_copy(0, m).start()

    @pl.loop(1, libs)
    def _(k):
        z_copy(k).start()

    @pl.loop(1, libs)
    def _(k):
        z_copy(k).wait_recv()

        @pl.loop(1, tmpls)
        def _(m):
            x_copy(k, m).start()

        s_copy(k, 0).start()

    @pl.loop(1, tmpls)
    def _(m):
        @pl.loop(0, libs)
        def _(k):
            x_copy(k, m).wait_recv()
            s_copy(k, m).start()

    @pl.loop(1, libs)
    def _(k):
        z_copy(k).wait_send()
        s_copy(k, 0).wait_send()
        s_copy(k, 0).wait_recv()

    @pl.loop(1, tmpls)
    def _(m):
        @pl.loop(0, libs)
        def _(k):
            x_copy(k, m).wait_send()
            s_copy(k, m).wait_send()
            s_copy(k, m).wait_recv()


def gather_blocks(xyz, charge, types, chans, owners, slots, libs, tmpls):
    dma = pltpu.SemaphoreType.DMA
    blocks = charge.shape[0]
    lead = (libs, tmpls)
    vmem = pl.BlockSpec(memory_space=pltpu.VMEM)
    return pl.pallas_call(
        functools.partial(gather_kernel, libs, tmpls),
        out_shape=(jax.ShapeDtypeStruct(lead + (4, blocks, 128), F32), jax.ShapeDtypeStruct(lead + (2, blocks, 128), jnp.int32),
                   jax.ShapeDtypeStruct(lead + (2,) + owners.shape, jnp.int32)),
        in_specs=[pl.BlockSpec(memory_space=pl.ANY)] * 6,
        out_specs=(vmem,) * 3,
        scratch_shapes=[dma((6,)), dma((libs, 3)), dma((libs, 3)), dma(lead + (3,)), dma(lead + (3,)),
                        dma(lead + (3,)), dma(lead + (3,))],
        compiler_params=pltpu.CompilerParams(collective_id=0, has_side_effects=True, vmem_limit_bytes=60 << 20),
    )(xyz, charge, types, chans, owners, slots)


def split3(a):
    h = a.astype(BF16).astype(F32)
    r = a - h
    m = r.astype(BF16).astype(F32)
    return h, m, r - m


def split2(a):
    h = a.astype(BF16)
    return h, (a - h.astype(F32)).astype(BF16)


def pair_kernel(me, name_ref, widths_ref, table_ref, real_ref, whole_ref, points_ref, bf_weights_ref, wg_ref, out_ref, res_ref,
                atom_ref, weights_ref):
    devices, _, per_dev, _ = real_ref.shape
    place = me()
    res_ref[...] = jnp.zeros_like(res_ref)
    row = lax.broadcasted_iota(jnp.int32, (8, 128), 0)
    row16 = lax.broadcasted_iota(jnp.int32, (VALUES, 128), 0)
    lane16 = lax.broadcasted_iota(jnp.int32, (VALUES, 128), 1)
    low = row < 4
    log2e = math.log2(math.e)
    wide = [widths_ref[f] for f in range(5)]
    scale = [-log2e * w for w in wide]

    @pl.loop(0, 5)
    def _(f):
        wg_ref[f] = jnp.zeros(wg_ref.shape[1:], F32)
        weights_ref[f] = bf_weights_ref[f].astype(F32)

    @pl.loop(0, devices)
    def _(dev):
        types = whole_ref[dev, 0]
        chan = whole_ref[dev, 1]
        steric = jnp.zeros(types.shape, F32)
        strength = jnp.zeros(types.shape, F32)
        for n in range(table_ref.shape[1]):
            same = types == n
            steric = jnp.where(same, table_ref[0, n], steric)
            strength = jnp.where(same, table_ref[1, n], strength)
        atom_ref[dev, 0] = steric
        atom_ref[dev, 1] = strength
        atom_ref[dev, 2] = jnp.where(chan == 0, scale[2], jnp.where(chan == 1, scale[3], scale[4]))

    def front(dev, b, slot):
        valid = jnp.where(slot >= 0, F32(1), F32(0))
        slot = jnp.maximum(slot, 0)
        here = pl.ds(b, 1)
        there = pl.ds(slot, 1)
        x = [jnp.broadcast_to(real_ref[dev, c, here, :], (8, 128)) for c in range(3)]
        y = [jnp.broadcast_to(points_ref[c, there, :], (8, 128)) for c in range(3)]
        chan = whole_ref[dev, 1, here, :]
        steric = atom_ref[dev, 0, here, :] * valid
        charge = real_ref[dev, 3, here, :] * valid
        strength = atom_ref[dev, 1, here, :] * valid
        pharm_scale = atom_ref[dev, 2, here, :]

        def rows(first, norm_row, one_row, p):
            norm = p[0] * p[0] + p[1] * p[1] + p[2] * p[2]
            v = jnp.where(row == 0, p[0] * first, jnp.where(row == 1, p[1] * first, p[2] * first))
            return jnp.where(row < 3, v, jnp.where(row == norm_row, norm, jnp.where(row == one_row, 1.0, 0.0)))

        def atom_side(v):
            h, m, l = split3(v)
            return jnp.concatenate([h, h, h, m, m, l], axis=0).astype(BF16)

        xv = rows(1.0, 3, 4, x)
        xs = atom_side(xv)
        yh, ym, yl = split3(rows(-2.0, 4, 3, y))
        ys = jnp.concatenate([yh, ym, yl, yh, ym, yh], axis=0).astype(BF16)
        if FLIP:
            both = jnp.concatenate([xs, atom_side(xv * pharm_scale)], axis=1)
            dist = lax.dot_general(both, ys, (((0,), (0,)), ((), ())), preferred_element_type=F32)
            dist, pharm = dist[:128], dist[128:]
        else:
            dist = lax.dot_general(ys, xs, (((0,), (0,)), ((), ())), preferred_element_type=F32)
            pharm = dist * pharm_scale
        inner = jnp.where(row % 4 == 0, 1.0, jnp.where(row % 4 == 1, x[0], jnp.where(row % 4 == 2, x[1], x[2])))
        outer = jnp.concatenate([jnp.where(low, 1.0, x[0]), jnp.where(low, x[1], x[2])], axis=0)
        moments = outer * jnp.concatenate([inner, inner], axis=0)

        return there, y, chan, steric, charge, strength, dist, pharm, moments

    def middle(there, y, chan, steric, charge, strength, dist, pharm, moments):
        def contract(exps, coefs):
            hi, lo = split2(exps)
            rhs = jnp.concatenate([hi, lo], axis=0 if FLIP else 1)
            lhs = jnp.concatenate([moments * c for c in coefs], axis=0)
            lh, ll = split2(lhs)
            lhs2 = jnp.concatenate([lh, ll], axis=0)
            lhs2 = jnp.concatenate([lhs2, lhs2], axis=1)
            got = lax.dot_general(lhs2, rhs, (((1,), (0 if FLIP else 1,)), ((), ())), preferred_element_type=F32)
            n = VALUES * len(coefs)
            got = got[:n] + got[n:]
            return [got[VALUES * c:VALUES * (c + 1)] for c in range(len(coefs))]

        parts = contract(jnp.exp2(dist * scale[0]), [steric]) + contract(jnp.exp2(dist * scale[1]), [charge])
        parts += contract(jnp.exp2(pharm), [jnp.where(chan == c, strength, 0.0) for c in range(3)])
        return there, y, parts

    def back(there, y, parts):
        total = jnp.zeros((VALUES, 128), F32)
        score = jnp.zeros((1, 128), F32)
        for f in range(5):
            v = weights_ref[f, there, :]
            score = score + v * parts[f][0:1]
            total = total + (v * (-2.0 * wide[f])) * parts[f]
        base = jnp.concatenate([total[0:4]] * 4, axis=0)
        y16 = jnp.concatenate([jnp.where(low, 0.0, y[0]), jnp.where(low, y[1], y[2])], axis=0)
        final = jnp.where(row16 == 0, score, total - y16 * base)
        summed = jnp.sum(final, axis=1, keepdims=True)
        return there, [p[0:1] for p in parts], summed

    group = math.gcd(GROUP, per_dev)

    @pl.loop(0, devices)
    def _(dev):
        @pl.loop(0, per_dev // group)
        def _(g):
            slots = []
            for u in range(group):
                slot = jnp.int32(-1)
                for k in range(name_ref.shape[2]):
                    slot = jnp.where(name_ref[dev, 0, k, g * group + u] == place, name_ref[dev, 1, k, g * group + u], slot)
                slots.append(slot)
            best = slots[0]
            for v in slots[1:]:
                best = jnp.maximum(best, v)

            @pl.when(best >= 0)
            def _():
                fronts, middles, done = {}, {}, []
                for u in range(group + 2 * SKEW):
                    if u < group:
                        fronts[u] = front(dev, g * group + u, slots[u])
                    if SKEW <= u < group + SKEW:
                        middles[u - SKEW] = middle(*fronts.pop(u - SKEW))
                    if u >= 2 * SKEW:
                        done.append(back(*middles.pop(u - 2 * SKEW)))
                for there, wparts, summed in done:
                    for f, part in enumerate(wparts):
                        wg_ref[f, there, :] += part
                acc = res_ref[dev]
                for u, (there, wparts, summed) in enumerate(done):
                    acc = jnp.where(lane16 == g * group + u, summed, acc)
                res_ref[dev] = acc

    @pl.loop(0, devices)
    def _(dev):
        r = res_ref[dev]
        packed = r[0:4]
        for q in range(1, 4):
            packed = packed + pltpu.roll(r[4 * q:4 * q + 4], 32 * q, 1)
        out_ref[dev] = packed


def run_pairs(me, names, widths, table, real, whole, points, weights):
    tmpl_count = points.shape[1]
    devices, _, per_dev, _ = real.shape
    vmem = pl.BlockSpec(memory_space=pltpu.VMEM)
    smem = pl.BlockSpec(memory_space=pltpu.SMEM)
    return pl.pallas_call(
        functools.partial(pair_kernel, me),
        out_shape=(jax.ShapeDtypeStruct((5, tmpl_count, 128), F32), jax.ShapeDtypeStruct((devices, 4, 128), F32)),
        in_specs=[smem, smem, smem, vmem, vmem, vmem, vmem],
        out_specs=(vmem, vmem),
        scratch_shapes=[pltpu.VMEM((devices, VALUES, 128), F32), pltpu.VMEM((devices, 3, per_dev, 128), F32),
                        pltpu.VMEM((5, tmpl_count, 128), F32)],
        compiler_params=pltpu.CompilerParams(vmem_limit_bytes=60 << 20, flags=FLAGS),
    )(names, widths, table, real, whole, points, weights)


def return_kernel(libs, tmpls, res_ref, owner_ref, score_ref, pose_ref, got_ref, local_sem, send_sem, recv_sem):
    l = lax.axis_index("lib")
    t = lax.axis_index("tmpl")
    s = lax.axis_index("sub")
    owners = libs * tmpls
    count = 2 * owners
    me = (l * tmpls + t) * 2 + s
    barrier = pltpu.get_barrier_semaphore()

    def peer(k):
        other = lax.rem(me + k, count)
        return other // 2, {"lib": other // (2 * tmpls), "tmpl": lax.rem(other // 2, tmpls), "sub": lax.rem(other, 2)}

    @pl.loop(1, count)
    def _(k):
        pl.semaphore_signal(barrier, inc=1, device_id=peer(k)[1], device_id_type=MESH)

    local = pltpu.make_async_copy(res_ref.at[l * tmpls + t], got_ref.at[me], local_sem)
    local.start()
    pl.semaphore_wait(barrier, count - 1)

    def copy(k):
        block, where = peer(k)
        return pltpu.make_async_remote_copy(
            src_ref=res_ref.at[block], dst_ref=got_ref.at[me], send_sem=send_sem.at[k], recv_sem=recv_sem.at[k],
            device_id=where, device_id_type=MESH)

    @pl.loop(1, count)
    def _(k):
        copy(k).start()

    local.wait()

    @pl.loop(1, count)
    def _(k):
        copy(k).wait()

    owner = owner_ref[...]
    per_block, blocks = owner.shape

    def add(o, carry):
        total, scores = carry
        both = got_ref[2 * o] + got_ref[2 * o + 1]
        scores = jnp.where(owner == o, jnp.broadcast_to(both[0:1, :blocks], (per_block, blocks)), scores)
        return total + both, scores

    total, scores = lax.fori_loop(0, owners, add, (jnp.zeros((4, 128), F32), jnp.zeros((per_block, blocks), F32)))
    rows = [total] + [pltpu.roll(total, 128 - 32 * q, 1) for q in range(1, 4)]
    pose = jnp.concatenate([rows[1][0:1], rows[2][0:1], rows[3][0:1], rows[1][1:4], rows[2][1:4], rows[3][1:4]], axis=0)
    score_ref[...] = scores
    pose_ref[...] = pose[:, :blocks]


def send_back(res, owner_rows, libs, tmpls):
    per_block, blocks = owner_rows.shape
    dma = pltpu.SemaphoreType.DMA
    count = 2 * libs * tmpls
    vmem = pl.BlockSpec(memory_space=pltpu.VMEM)
    return pl.pallas_call(
        functools.partial(return_kernel, libs, tmpls),
        out_shape=(jax.ShapeDtypeStruct((per_block, blocks), F32), jax.ShapeDtypeStruct((12, blocks), F32)),
        in_specs=[vmem, vmem],
        out_specs=(vmem, vmem),
        scratch_shapes=[pltpu.VMEM((count, 4, 128), F32), dma, dma((count,)), dma((count,))],
        compiler_params=pltpu.CompilerParams(collective_id=1, has_side_effects=True),
    )(res, owner_rows)


def local(libs, tmpls, coords, atom_type, channel, charge, pair_owner, pair_slot, type_table, widths, tmpl_points,
          tmpl_weights):
    owners, slots = pair_owner.T, pair_slot.T
    real, whole, names = gather_blocks(jnp.transpose(coords, (1, 0, 2)), charge, atom_type, channel, owners, slots, libs, tmpls)
    count = libs * tmpls
    real, whole, names = [a.reshape((count,) + a.shape[2:]) for a in (real, whole, names)]

    def me():
        return lax.axis_index("lib") * tmpls + lax.axis_index("tmpl")

    weight_grad, res = run_pairs(me, names, widths, type_table.T, real, whole, jnp.transpose(tmpl_points, (1, 0, 2)),
                                 jnp.transpose(tmpl_weights, (1, 0, 2)))
    scores, pose = send_back(res, owners, libs, tmpls)
    return scores.T, pose.T, jnp.transpose(weight_grad, (1, 0, 2))


def solution(mesh):
    every = ("groups", "lib", "tmpl")
    in_specs = (P(every, None, None), P(every, None), P(every, None), P(every, None), P(every, None), P(every, None),
                P(), P(), P(("lib", "tmpl"), None, "sub"), P(("lib", "tmpl"), None, "sub"))
    out_specs = (P(every, None), P(every, None), P(every, None, "sub"))
    body = functools.partial(local, mesh.shape["lib"], mesh.shape["tmpl"])
    return jax.shard_map(body, mesh=mesh, in_specs=in_specs, out_specs=out_specs, check_vma=False)
```
